32 devices in a mesh: wide: 8 (over z, x), narrow: 4 (over y, core).
Axes of the slice: x: 2, y: 2, z: 4, core: 2. Of those that a mesh axis runs over, the one named last changes fastest.
Arguments:
- state: float32 [2, 2097152], P(None, ('wide', 'narrow')), may hold values from -6 to 6
- gates: float32 [8, 2, 128, 128], replicated, may hold values from -1 to 1, as said below
- gate_qubits: int32 [8, 7], replicated, may hold values from 7 to 15, as said below
- swap_order: int32 [9], replicated, may hold values from 7 to 15, as said below
Outputs:
- checkpoint: float32 [2, 2097152], P(None, ('wide', 'narrow'))
The draws below stay inside these ranges and needn't reach their ends.
Inputs may be any that keep to these rules, and one draw needn't show every extreme that they name: `gate_qubits`: each row names 7 different qubits. `swap_order`: each number of the range appears once. Each gates[g, 0] + i gates[g, 1] is a unitary matrix.
All inputs are finite; a program needn't handle non-finite values.
Results may differ from the reference program's by a relative error of at most 0.0003.
Values sent between devices are 32-bit elements; how exact they have to be, the bound alone decides.
A program may use at most 64 MiB of HBM per device.

```python
import math
import jax
import jax.numpy as jnp
from jax import lax

AMP_DEV = 65536
GATE_QUBITS = 7
LANE_QUBITS = 7
GATES = 8
GATE_DIM = 128
LOCAL_QUBITS = 16
NAMPS = 2097152
N_WIDE = 8
N_NARROW = 4


def orthonormal(matrix_pair):
    source_real = matrix_pair[0]
    source_imag = matrix_pair[1]
    extent = source_real.shape[0]

    def column_step(column, frames):
        frame_real, frame_imag = frames
        vector_real = lax.dynamic_index_in_dim(source_real, column, 1, keepdims=False)
        vector_imag = lax.dynamic_index_in_dim(source_imag, column, 1, keepdims=False)
        for repeat in range(2):
            weight_real = jnp.dot(frame_real.T, vector_real, precision=lax.Precision.HIGHEST) + jnp.dot(frame_imag.T, vector_imag, precision=lax.Precision.HIGHEST)
            weight_imag = jnp.dot(frame_real.T, vector_imag, precision=lax.Precision.HIGHEST) - jnp.dot(frame_imag.T, vector_real, precision=lax.Precision.HIGHEST)
            vector_real = vector_real - (jnp.dot(frame_real, weight_real, precision=lax.Precision.HIGHEST) - jnp.dot(frame_imag, weight_imag, precision=lax.Precision.HIGHEST))
            vector_imag = vector_imag - (jnp.dot(frame_real, weight_imag, precision=lax.Precision.HIGHEST) + jnp.dot(frame_imag, weight_real, precision=lax.Precision.HIGHEST))
        length = jnp.sqrt(jnp.sum(vector_real * vector_real + vector_imag * vector_imag))
        frame_real = lax.dynamic_update_index_in_dim(frame_real, vector_real / length, column, 1)
        frame_imag = lax.dynamic_update_index_in_dim(frame_imag, vector_imag / length, column, 1)
        return (frame_real, frame_imag)
    zeros_block = jnp.zeros((extent, extent), jnp.float32)
    frames = lax.fori_loop(0, extent, column_step, (zeros_block, zeros_block))
    return jnp.stack([frames[0], frames[1]])


def draw_gates(key, part):
    samples = jax.random.normal(jax.random.fold_in(key, 5), (GATES, 2, GATE_DIM, GATE_DIM), jnp.float32)
    return jax.vmap(orthonormal)(samples).astype(jnp.float32)


def draw_gate_qubits(key, part):
    subkeys = jax.random.split(jax.random.fold_in(key, 11), GATES)
    upper_count = LOCAL_QUBITS - LANE_QUBITS
    chosen = jax.vmap(lambda single: jax.random.permutation(single, upper_count)[:GATE_QUBITS])(subkeys)
    return (chosen + LANE_QUBITS).astype(jnp.int32)


def draw_swap_order(key, part):
    upper_count = LOCAL_QUBITS - LANE_QUBITS
    ordering = jax.random.permutation(jax.random.fold_in(key, 17), upper_count)
    return (ordering + LANE_QUBITS).astype(jnp.int32)


def level_of(key, dims, cuts, low, high):
    gain = 1.0
    for dim, blocks in cuts:
        steps = jax.random.uniform(jax.random.fold_in(jax.random.fold_in(key, 6), dim), (blocks,), jnp.float32, low / len(cuts), high / len(cuts))
        gain = gain * jnp.repeat(jnp.exp(steps), dims[dim] // blocks).reshape((-1,) + (1,) * (len(dims) - 1 - dim))
    return gain


def noise(key, shape, spread, most, shards=(), kind=jnp.bfloat16):
    array = jax.random.normal(key, shape, jnp.float32) * spread
    if len(shards) > 0:
        array = level_of(key, shape, shards, -0.22, 0.18) * array
    return jnp.clip(array, min=-most, max=most).astype(kind)


def setup_inputs(seed: int = 0) -> dict:
    keys = jax.random.split(jax.random.key(seed), 5)
    return {
        "state": noise(keys[0], (2, NAMPS), 1.0, 6.0, ((1, 32),), jnp.float32),
        "gates": draw_gates(jax.random.fold_in(keys[4], 71), 0),
        "gate_qubits": draw_gate_qubits(jax.random.fold_in(keys[4], 71), 0),
        "swap_order": draw_swap_order(jax.random.fold_in(keys[4], 71), 0),
    }


companding = 16.0
companding_norm = math.log(16.0 + math.sqrt(257.0))

def inverse_sinh(values):
    magnitude = jnp.abs(values)
    squared = magnitude * magnitude
    return jnp.sign(values) * jnp.log1p(magnitude + squared / (1.0 + jnp.sqrt(squared + 1.0)))

def shuffle_index(source, target, qubit_count):
    position = jnp.argsort(source).astype(jnp.int32)
    shifts = position[target].astype(jnp.int32)
    low_count = qubit_count // 2
    high_count = qubit_count - low_count
    low_values = jnp.arange(2 ** low_count, dtype=jnp.int32)
    high_values = jnp.arange(2 ** high_count, dtype=jnp.int32)
    low_bits = jnp.right_shift(low_values[:, None], jnp.arange(low_count, dtype=jnp.int32)[None, :]) & 1
    high_bits = jnp.right_shift(high_values[:, None], jnp.arange(high_count, dtype=jnp.int32)[None, :]) & 1
    low_part = lax.optimization_barrier(jnp.sum(jnp.left_shift(low_bits, shifts[None, :low_count]), axis=1)).astype(jnp.int32)
    high_part = lax.optimization_barrier(jnp.sum(jnp.left_shift(high_bits, shifts[None, low_count:]), axis=1)).astype(jnp.int32)
    return (high_part[:, None] + low_part[None, :]).reshape(-1).astype(jnp.int32)

def gate_order(chosen, qubit_count):
    ranking = jnp.arange(qubit_count, dtype=jnp.int32) + qubit_count
    ranking = ranking.at[chosen].set(jnp.arange(chosen.shape[0], dtype=jnp.int32))
    return jnp.argsort(ranking).astype(jnp.int32)

def top_order(chosen, qubit_count):
    ranking = jnp.arange(qubit_count, dtype=jnp.int32)
    ranking = ranking.at[chosen].set(qubit_count + jnp.arange(chosen.shape[0], dtype=jnp.int32))
    return jnp.argsort(ranking).astype(jnp.int32)

def gate_blocks(matrix):
    real_part = matrix[0]
    imag_part = matrix[1]
    return jnp.stack([jnp.stack([real_part, imag_part]), jnp.stack([-imag_part, real_part])])

def apply_local(values, matrix):
    shaped = values.reshape(2, -1, matrix.shape[-1])
    mixed = jnp.einsum('crb,cdab->dra', shaped, gate_blocks(matrix), precision=lax.Precision.HIGHEST)
    return mixed.reshape(values.shape)

def reference_gate(amplitudes, matrix, chosen):
    natural = jnp.arange(LOCAL_QUBITS, dtype=jnp.int32)
    layout = gate_order(chosen, LOCAL_QUBITS)
    arranged = jnp.take(amplitudes, shuffle_index(natural, layout, LOCAL_QUBITS), axis=2)
    mixed = apply_local(arranged, matrix)
    return jnp.take(mixed, shuffle_index(layout, natural, LOCAL_QUBITS), axis=2)

def reference_swap(amplitudes, chosen, group_count, first_axis):
    natural = jnp.arange(LOCAL_QUBITS, dtype=jnp.int32)
    layout = top_order(chosen, LOCAL_QUBITS)
    arranged = jnp.take(amplitudes, shuffle_index(natural, layout, LOCAL_QUBITS), axis=2)
    grid = arranged.reshape(2, N_WIDE, N_NARROW, group_count, AMP_DEV // group_count)
    grid = jnp.swapaxes(grid, first_axis, 3)
    arranged = grid.reshape(2, N_WIDE * N_NARROW, AMP_DEV)
    return jnp.take(arranged, shuffle_index(layout, natural, LOCAL_QUBITS), axis=2)

def reference(state, gates, gate_qubits, swap_order):
    wide_bits = N_WIDE.bit_length() - 1
    narrow_bits = N_NARROW.bit_length() - 1
    upper_count = LOCAL_QUBITS - LANE_QUBITS
    amplitudes = state.reshape(2, N_WIDE * N_NARROW, AMP_DEV)
    for number in range(3):
        amplitudes = reference_gate(amplitudes, gates[number], gate_qubits[number])
    amplitudes = reference_swap(amplitudes, swap_order[upper_count - wide_bits:], N_WIDE, 1)
    for number in range(3, 6):
        amplitudes = reference_gate(amplitudes, gates[number], gate_qubits[number])
    amplitudes = reference_swap(amplitudes, swap_order[:narrow_bits], N_NARROW, 2)
    for number in range(6, 8):
        amplitudes = reference_gate(amplitudes, gates[number], gate_qubits[number])
    final = amplitudes.reshape(2, -1)
    highest = jnp.max(final)
    lowest = jnp.min(final)
    middle = (highest + lowest) * 0.5
    halfwidth = (highest - lowest) * 0.5 + 1e-06
    return inverse_sinh(companding * (final - middle) / halfwidth) / companding_norm
```

```python
import functools
import math

import jax
import jax.numpy as jnp
from jax import lax
from jax.experimental import pallas as pl
from jax.experimental.pallas import tpu as pltpu
from jax.sharding import PartitionSpec as P

LANE_QUBITS = 7
LANES = 2**LANE_QUBITS
CHUNKS = 2

companding = 16.0
companding_norm = math.log(16.0 + math.sqrt(257.0))

MESH = pl.DeviceIdType.MESH


def inverse_sinh(values):
    magnitude = jnp.abs(values)
    squared = magnitude * magnitude
    return jnp.sign(values) * jnp.log1p(magnitude + squared / (1.0 + jnp.sqrt(squared + 1.0)))


def kernel(
    n_wide,
    n_narrow,
    upper,
    gate_bits,
    stages,
    qubits_ref,
    swap_ref,
    state_ref,
    gates_ref,
    final_ref,
    ext_ref,
    state_v,
    gates_v,
    final_v,
    perms,
    mats,
    wide_out,
    wide_in,
    narrow_out,
    narrow_in,
    ext_out,
    ext_narrow,
    ext_mid,
    ext_wide,
    local_sem,
    gate_sem,
    wide_send,
    wide_recv,
    narrow_send,
    narrow_recv,
    ext_nsend,
    ext_nrecv,
    ext_wsend,
    ext_wrecv,
):
    rows = 2**upper
    gate_dim = 2**gate_bits
    rest = rows // gate_dim
    wide_bits = n_wide.bit_length() - 1
    narrow_bits = n_narrow.bit_length() - 1
    wide_me = lax.axis_index("wide")
    narrow_me = lax.axis_index("narrow")
    half = LANES // 2

    state_copy = pltpu.make_async_copy(state_ref, state_v, local_sem.at[0])
    state_copy.start()
    gate_copies = []
    for number in range(gates_v.shape[0]):
        copy = pltpu.make_async_copy(
            gates_ref.at[number], gates_v.at[number], gate_sem.at[number]
        )
        copy.start()
        gate_copies.append(copy)

    barrier = pltpu.get_barrier_semaphore()
    for apart in range(1, n_wide):
        pl.semaphore_signal(
            barrier,
            inc=1,
            device_id=(lax.rem(wide_me + apart, n_wide), narrow_me),
            device_id_type=MESH,
        )
    for apart in range(1, n_narrow):
        pl.semaphore_signal(
            barrier,
            inc=1,
            device_id=(wide_me, lax.rem(narrow_me + apart, n_narrow)),
            device_id_type=MESH,
        )

    def gate_layout(number):
        masks = [jnp.int32(1) << (qubits_ref[number, k] - LANE_QUBITS) for k in range(gate_bits)]
        left = jnp.int32(rows - 1)
        for mask in masks:
            left = left - mask
        for _ in range(upper - gate_bits):
            low = left & (-left)
            masks.append(low)
            left = left - low
        return masks

    def swap_layout(order):
        return [jnp.int32(1) << (swap_ref[k] - LANE_QUBITS) for k in order]

    natural = [jnp.int32(1 << k) for k in range(upper)]
    wide_layout = swap_layout(range(upper))
    narrow_layout = swap_layout(list(range(narrow_bits, upper)) + list(range(narrow_bits)))

    column = lax.broadcasted_iota(jnp.int32, (1, rows), 1)
    row = lax.broadcasted_iota(jnp.int32, (rows, rows), 0)

    def make_perm(slot, source, target):
        index = jnp.zeros((1, rows), jnp.int32)
        for k in range(upper):
            index = index + jnp.where((column & (1 << k)) != 0, source[k], 0)
        goal = jnp.zeros((1, rows), jnp.int32)
        for k in range(upper):
            goal = goal + jnp.where((index & target[k]) != 0, 1 << k, 0)
        perms[slot] = (row == goal).astype(jnp.float32).astype(jnp.bfloat16)

    def make_matrix(number):
        gate_copies[number].wait()
        whole = jnp.concatenate([gates_v[number, 0], gates_v[number, 1]], axis=1)
        high = whole.astype(jnp.bfloat16)
        low = (whole - high.astype(jnp.float32)).astype(jnp.bfloat16)
        mats[number, :gate_dim] = high
        mats[number, gate_dim:] = low

    sign = jnp.where(lax.broadcasted_iota(jnp.int32, (1, LANES), 1) < half, -1.0, 1.0)

    def permuted(values, slot):
        high = values.astype(jnp.bfloat16)
        low = (values - high.astype(jnp.float32)).astype(jnp.bfloat16)
        both = jnp.concatenate([high, low], axis=1)
        moved = jnp.dot(perms[slot], both, preferred_element_type=jnp.float32)
        return moved[:, :LANES], moved[:, LANES:]

    def stacked(values):
        turned = pltpu.roll(values, half, 1) * sign
        pieces = []
        for part in (values, turned):
            pieces.append(
                jnp.concatenate(
                    [part[k * gate_dim : (k + 1) * gate_dim] for k in range(rest)], axis=1
                ).astype(jnp.bfloat16)
            )
        return jnp.concatenate(pieces, axis=0)

    def gate(values, slot, number):
        high, low = permuted(values, slot)
        first = jnp.dot(mats[number], stacked(high), preferred_element_type=jnp.float32)
        second = jnp.dot(
            mats[number, :gate_dim], stacked(low), preferred_element_type=jnp.float32
        )
        mixed = first[:gate_dim] + (first[gate_dim:] + second)
        return jnp.concatenate(
            [mixed[:, k * LANES : (k + 1) * LANES] for k in range(rest)], axis=0
        )

    def moved(values, slot):
        high, low = permuted(values, slot)
        return high + low

    def wide_copy(chunk, apart):
        other = lax.rem(wide_me + apart, n_wide)
        return pltpu.make_async_remote_copy(
            src_ref=wide_out.at[chunk, other],
            dst_ref=wide_in.at[chunk, wide_me],
            send_sem=wide_send.at[chunk, apart - 1],
            recv_sem=wide_recv.at[chunk, apart - 1],
            device_id=(other, narrow_me),
            device_id_type=MESH,
        )

    def narrow_copy(chunk, apart):
        other = lax.rem(narrow_me + apart, n_narrow)
        return pltpu.make_async_remote_copy(
            src_ref=narrow_out.at[chunk, other],
            dst_ref=narrow_in.at[chunk, narrow_me],
            send_sem=narrow_send.at[chunk, apart - 1],
            recv_sem=narrow_recv.at[chunk, apart - 1],
            device_id=(wide_me, other),
            device_id_type=MESH,
        )

    slot = 0
    plan = []
    for numbers, leave in zip(stages, (wide_layout, narrow_layout, natural)):
        plan.append((slot, numbers, leave))
        slot += len(numbers) + 1

    def prepare(stage, layout):
        start, numbers, leave = plan[stage]
        for k, number in enumerate(numbers):
            target = gate_layout(number)
            make_perm(start + k, layout, target)
            make_matrix(number)
            layout = target
        make_perm(start + len(numbers), layout, leave)

    def run(values, stage):
        start, numbers, _ = plan[stage]
        for k, number in enumerate(numbers):
            values = gate(values, start + k, number)
        return moved(values, start + len(numbers))

    prepare(0, natural)
    state_copy.wait()
    real = state_v[pl.ds(0, rows, stride=2), :]
    imag = state_v[pl.ds(1, rows, stride=2), :]
    first_half = lax.broadcasted_iota(jnp.int32, (1, LANES), 1) < half
    pieces = (
        jnp.where(first_half, real, pltpu.roll(imag, half, 1)),
        jnp.where(first_half, pltpu.roll(real, half, 1), imag),
    )
    for chunk in range(CHUNKS):
        values = run(pieces[chunk], 0)
        wide_out[chunk] = values.reshape(n_wide, rows // n_wide, LANES)
        if chunk == 0:
            pl.semaphore_wait(barrier, n_wide + n_narrow - 2)
        for apart in range(1, n_wide):
            wide_copy(chunk, apart).start()
        wide_in[chunk, wide_me] = wide_out[chunk, wide_me]

    prepare(1, wide_layout)
    prepare(2, narrow_layout)
    for chunk in range(CHUNKS):
        for apart in range(1, n_wide):
            wide_copy(chunk, apart).wait_recv()
        values = run(wide_in[chunk].reshape(rows, LANES), 1)
        narrow_out[chunk] = values.reshape(n_narrow, rows // n_narrow, LANES)
        for apart in range(1, n_narrow):
            narrow_copy(chunk, apart).start()
        narrow_in[chunk, narrow_me] = narrow_out[chunk, narrow_me]

    results = []
    for chunk in range(CHUNKS):
        for apart in range(1, n_narrow):
            narrow_copy(chunk, apart).wait_recv()
        results.append(run(narrow_in[chunk].reshape(rows, LANES), 2))

    high = jnp.maximum(results[0], results[1]).reshape(rows // 8, 8, LANES).max(axis=0)
    low = jnp.minimum(results[0], results[1]).reshape(rows // 8, 8, LANES).min(axis=0)
    ext_out[0] = high
    ext_out[1] = -low

    def ext_narrow_copy(apart):
        return pltpu.make_async_remote_copy(
            src_ref=ext_out,
            dst_ref=ext_narrow.at[apart - 1],
            send_sem=ext_nsend.at[apart - 1],
            recv_sem=ext_nrecv.at[apart - 1],
            device_id=(wide_me, lax.rem(narrow_me + apart, n_narrow)),
            device_id_type=MESH,
        )

    def ext_wide_copy(apart):
        return pltpu.make_async_remote_copy(
            src_ref=ext_mid,
            dst_ref=ext_wide.at[apart - 1],
            send_sem=ext_wsend.at[apart - 1],
            recv_sem=ext_wrecv.at[apart - 1],
            device_id=(lax.rem(wide_me + apart, n_wide), narrow_me),
            device_id_type=MESH,
        )

    for apart in range(1, n_narrow):
        ext_narrow_copy(apart).start()
    first_half_final, second_half_final = results
    final_v[pl.ds(0, rows, stride=2), :] = jnp.where(
        first_half, first_half_final, pltpu.roll(second_half_final, half, 1)
    )
    final_v[pl.ds(1, rows, stride=2), :] = jnp.where(
        first_half, pltpu.roll(first_half_final, half, 1), second_half_final
    )
    final_copy = pltpu.make_async_copy(final_v, final_ref, local_sem.at[1])
    final_copy.start()
    total = ext_out[...]
    for apart in range(1, n_narrow):
        ext_narrow_copy(apart).wait_recv()
        total = jnp.maximum(total, ext_narrow[apart - 1])
    ext_mid[...] = total
    for apart in range(1, n_wide):
        ext_wide_copy(apart).start()
    for apart in range(1, n_wide):
        ext_wide_copy(apart).wait_recv()
        total = jnp.maximum(total, ext_wide[apart - 1])
    ext_ref[0:1] = jnp.full((1, LANES), jnp.max(total[0]))
    ext_ref[1:2] = jnp.full((1, LANES), jnp.max(total[1]))

    for chunk in range(CHUNKS):
        for apart in range(1, n_wide):
            wide_copy(chunk, apart).wait_send()
        for apart in range(1, n_narrow):
            narrow_copy(chunk, apart).wait_send()
    for apart in range(1, n_narrow):
        ext_narrow_copy(apart).wait_send()
    for apart in range(1, n_wide):
        ext_wide_copy(apart).wait_send()
    final_copy.wait()


def local(state, gates, gate_qubits, swap_order):
    n_wide = lax.axis_size("wide")
    n_narrow = lax.axis_size("narrow")
    upper = state.shape[1].bit_length() - 1 - LANE_QUBITS
    rows = 2**upper
    gate_count, gate_bits = gate_qubits.shape
    gate_dim = 2**gate_bits
    stages = (range(3), range(3, 6), range(6, gate_count))
    dma = pltpu.SemaphoreType.DMA
    woven = state.reshape(2, rows, LANES).transpose(1, 0, 2).reshape(2 * rows, LANES)
    final, extremes = pl.pallas_call(
        functools.partial(kernel, n_wide, n_narrow, upper, gate_bits, stages),
        out_shape=(
            jax.ShapeDtypeStruct((2 * rows, LANES), jnp.float32),
            jax.ShapeDtypeStruct((2, LANES), jnp.float32),
        ),
        in_specs=[
            pl.BlockSpec(memory_space=pltpu.SMEM),
            pl.BlockSpec(memory_space=pltpu.SMEM),
            pl.BlockSpec(memory_space=pl.ANY),
            pl.BlockSpec(memory_space=pl.ANY),
        ],
        out_specs=(
            pl.BlockSpec(memory_space=pl.ANY),
            pl.BlockSpec(memory_space=pltpu.VMEM),
        ),
        scratch_shapes=[
            pltpu.VMEM((2 * rows, LANES), jnp.float32),
            pltpu.VMEM(gates.shape, jnp.float32),
            pltpu.VMEM((2 * rows, LANES), jnp.float32),
            pltpu.VMEM((gate_count + 3, rows, rows), jnp.bfloat16),
            pltpu.VMEM((gate_count, 2 * gate_dim, 2 * gate_dim), jnp.bfloat16),
            pltpu.VMEM((CHUNKS, n_wide, rows // n_wide, LANES), jnp.float32),
            pltpu.VMEM((CHUNKS, n_wide, rows // n_wide, LANES), jnp.float32),
            pltpu.VMEM((CHUNKS, n_narrow, rows // n_narrow, LANES), jnp.float32),
            pltpu.VMEM((CHUNKS, n_narrow, rows // n_narrow, LANES), jnp.float32),
            pltpu.VMEM((2, 8, LANES), jnp.float32),
            pltpu.VMEM((n_narrow - 1, 2, 8, LANES), jnp.float32),
            pltpu.VMEM((2, 8, LANES), jnp.float32),
            pltpu.VMEM((n_wide - 1, 2, 8, LANES), jnp.float32),
            dma((2,)),
            dma((gate_count,)),
            dma((CHUNKS, n_wide - 1)),
            dma((CHUNKS, n_wide - 1)),
            dma((CHUNKS, n_narrow - 1)),
            dma((CHUNKS, n_narrow - 1)),
            dma((n_narrow - 1,)),
            dma((n_narrow - 1,)),
            dma((n_wide - 1,)),
            dma((n_wide - 1,)),
        ],
        compiler_params=pltpu.CompilerParams(
            collective_id=0, has_side_effects=True, vmem_limit_bytes=48 * 2**20
        ),
        name="gate_layers",
    )(gate_qubits, swap_order, woven, gates)
    final = final.reshape(rows, 2, LANES).transpose(1, 0, 2).reshape(state.shape)
    highest = extremes[0, 0]
    lowest = -extremes[1, 0]
    middle = (highest + lowest) * 0.5
    halfwidth = (highest - lowest) * 0.5 + 1e-06
    return inverse_sinh(companding * (final - middle) / halfwidth) / companding_norm


def solution(mesh):
    in_specs = (P(None, ("wide", "narrow")), P(), P(), P())
    out_specs = P(None, ("wide", "narrow"))
    return jax.shard_map(local, mesh=mesh, in_specs=in_specs, out_specs=out_specs, check_vma=False)
```

```python
import functools
import math

import jax
import jax.numpy as jnp
from jax import lax
from jax.experimental import pallas as pl
from jax.experimental.pallas import tpu as pltpu
from jax.sharding import PartitionSpec as P

LANE_QUBITS = 7
LANES = 2**LANE_QUBITS
CHUNKS = 2

companding = 16.0
companding_norm = math.log(16.0 + math.sqrt(257.0))

MESH = pl.DeviceIdType.MESH


def kernel(
    n_wide,
    n_narrow,
    upper,
    gate_bits,
    stages,
    qubits_hbm,
    swap_hbm,
    state_ref,
    gates_ref,
    out_ref,
    qubits_ref,
    swap_ref,
    state_v,
    gates_v,
    perms,
    mats,
    wide_out,
    wide_in,
    narrow_out,
    narrow_in,
    ext_out,
    ext_in,
    local_sem,
    gate_sem,
    wide_send,
    wide_recv,
    narrow_send,
    narrow_recv,
    ext_send,
    ext_recv,
):
    rows = 2**upper
    gate_dim = 2**gate_bits
    rest = rows // gate_dim
    wide_bits = n_wide.bit_length() - 1
    narrow_bits = n_narrow.bit_length() - 1
    wide_me = lax.axis_index("wide")
    narrow_me = lax.axis_index("narrow")
    half = LANES // 2

    qubits_copy = pltpu.make_async_copy(qubits_hbm, qubits_ref, local_sem.at[1])
    qubits_copy.start()
    swap_copy = pltpu.make_async_copy(swap_hbm, swap_ref, local_sem.at[2])
    swap_copy.start()
    state_copy = pltpu.make_async_copy(state_ref, state_v, local_sem.at[0])
    state_copy.start()
    gate_copies = []
    for number in range(gates_v.shape[0]):
        copy = pltpu.make_async_copy(
            gates_ref.at[number], gates_v.at[number], gate_sem.at[number]
        )
        copy.start()
        gate_copies.append(copy)

    barrier = pltpu.get_barrier_semaphore()
    devices = n_wide * n_narrow
    flat_me = wide_me * n_narrow + narrow_me

    def device_at(apart):
        other = lax.rem(flat_me + apart, devices)
        return (lax.div(other, n_narrow), lax.rem(other, n_narrow))

    def for_others(step):
        if devices <= 64:
            for apart in range(1, devices):
                step(apart)
        else:
            lax.fori_loop(1, devices, lambda apart, _: step(apart), None)

    def greet(apart):
        pl.semaphore_signal(barrier, inc=1, device_id=device_at(apart), device_id_type=MESH)

    for_others(greet)
    qubits_copy.wait()
    swap_copy.wait()

    def gate_layout(number):
        masks = [jnp.int32(1) << (qubits_ref[number, k] - LANE_QUBITS) for k in range(gate_bits)]
        left = jnp.int32(rows - 1)
        for mask in masks:
            left = left - mask
        for _ in range(upper - gate_bits):
            low = left & (-left)
            masks.append(low)
            left = left - low
        return masks

    def swap_layout(order):
        return [jnp.int32(1) << (swap_ref[k] - LANE_QUBITS) for k in order]

    natural = [jnp.int32(1 << k) for k in range(upper)]
    wide_layout = swap_layout(range(upper))
    narrow_layout = swap_layout(list(range(narrow_bits, upper)) + list(range(narrow_bits)))

    column = lax.broadcasted_iota(jnp.int32, (1, rows), 1)
    row = lax.broadcasted_iota(jnp.int32, (rows, rows), 0)

    def make_perm(slot, source, target):
        index = jnp.zeros((1, rows), jnp.int32)
        for k in range(upper):
            index = index + jnp.where((column & (1 << k)) != 0, source[k], 0)
        goal = jnp.zeros((1, rows), jnp.int32)
        for k in range(upper):
            goal = goal + jnp.where((index & target[k]) != 0, 1 << k, 0)
        perms[slot] = (row == goal).astype(jnp.float32).astype(jnp.bfloat16)

    def make_matrix(number):
        gate_copies[number].wait()
        whole = jnp.concatenate([gates_v[number, 0], gates_v[number, 1]], axis=1)
        high = whole.astype(jnp.bfloat16)
        low = (whole - high.astype(jnp.float32)).astype(jnp.bfloat16)
        mats[number, :gate_dim] = high
        mats[number, gate_dim:] = low

    sign = jnp.where(lax.broadcasted_iota(jnp.int32, (1, LANES), 1) < half, -1.0, 1.0)

    def permuted(values, slot):
        high = values.astype(jnp.bfloat16)
        low = (values - high.astype(jnp.float32)).astype(jnp.bfloat16)
        both = jnp.concatenate([high, low], axis=1)
        moved = jnp.dot(perms[slot], both, preferred_element_type=jnp.float32)
        return moved[:, :LANES], moved[:, LANES:]

    def stacked(values):
        turned = pltpu.roll(values, half, 1) * sign
        pieces = []
        for part in (values, turned):
            pieces.append(
                jnp.concatenate(
                    [part[k * gate_dim : (k + 1) * gate_dim] for k in range(rest)], axis=1
                ).astype(jnp.bfloat16)
            )
        return jnp.concatenate(pieces, axis=0)

    def gate(values, slot, number):
        high, low = permuted(values, slot)
        first = jnp.dot(mats[number], stacked(high), preferred_element_type=jnp.float32)
        second = jnp.dot(
            mats[number, :gate_dim], stacked(low), preferred_element_type=jnp.float32
        )
        mixed = first[:gate_dim] + (first[gate_dim:] + second)
        return jnp.concatenate(
            [mixed[:, k * LANES : (k + 1) * LANES] for k in range(rest)], axis=0
        )

    def moved(values, slot):
        high, low = permuted(values, slot)
        return high + low

    def wide_copy(chunk, apart):
        other = lax.rem(wide_me + apart, n_wide)
        return pltpu.make_async_remote_copy(
            src_ref=wide_out.at[chunk, other],
            dst_ref=wide_in.at[chunk, wide_me],
            send_sem=wide_send.at[chunk, apart - 1],
            recv_sem=wide_recv.at[chunk, apart - 1],
            device_id=(other, narrow_me),
            device_id_type=MESH,
        )

    def narrow_copy(chunk, apart):
        other = lax.rem(narrow_me + apart, n_narrow)
        return pltpu.make_async_remote_copy(
            src_ref=narrow_out.at[chunk, other],
            dst_ref=narrow_in.at[chunk, narrow_me],
            send_sem=narrow_send.at[chunk, apart - 1],
            recv_sem=narrow_recv.at[chunk, apart - 1],
            device_id=(wide_me, other),
            device_id_type=MESH,
        )

    slot = 0
    plan = []
    for numbers, leave in zip(stages, (wide_layout, narrow_layout, natural)):
        plan.append((slot, numbers, leave))
        slot += len(numbers) + 1

    def prepare(stage, layout):
        start, numbers, leave = plan[stage]
        for k, number in enumerate(numbers):
            target = gate_layout(number)
            make_perm(start + k, layout, target)
            make_matrix(number)
            layout = target
        make_perm(start + len(numbers), layout, leave)

    def run(values, stage):
        start, numbers, _ = plan[stage]
        for k, number in enumerate(numbers):
            values = gate(values, start + k, number)
        return moved(values, start + len(numbers))

    prepare(0, natural)
    state_copy.wait()
    real = state_v[pl.ds(0, rows, stride=2), :]
    imag = state_v[pl.ds(1, rows, stride=2), :]
    first_half = lax.broadcasted_iota(jnp.int32, (1, LANES), 1) < half
    pieces = (
        jnp.where(first_half, real, pltpu.roll(imag, half, 1)),
        jnp.where(first_half, pltpu.roll(real, half, 1), imag),
    )
    for chunk in range(CHUNKS):
        values = run(pieces[chunk], 0)
        wide_out[chunk] = values.reshape(n_wide, rows // n_wide, LANES)
        if chunk == 0:
            pl.semaphore_wait(barrier, devices - 1)
        for apart in range(1, n_wide):
            wide_copy(chunk, apart).start()
        wide_in[chunk, wide_me] = wide_out[chunk, wide_me]

    prepare(1, wide_layout)
    prepare(2, narrow_layout)
    for chunk in range(CHUNKS):
        for apart in range(1, n_wide):
            wide_copy(chunk, apart).wait_recv()
        values = run(wide_in[chunk].reshape(rows, LANES), 1)
        narrow_out[chunk] = values.reshape(n_narrow, rows // n_narrow, LANES)
        for apart in range(1, n_narrow):
            narrow_copy(chunk, apart).start()
        narrow_in[chunk, narrow_me] = narrow_out[chunk, narrow_me]

    results = []
    for chunk in range(CHUNKS):
        for apart in range(1, n_narrow):
            narrow_copy(chunk, apart).wait_recv()
        results.append(run(narrow_in[chunk].reshape(rows, LANES), 2))

    high = jnp.maximum(results[0], results[1]).max(axis=0, keepdims=True)
    low = -jnp.minimum(results[0], results[1]).min(axis=0, keepdims=True)
    high = jnp.maximum(high, pltpu.roll(high, half, 1))
    low = jnp.maximum(low, pltpu.roll(low, half, 1))
    ext_out[...] = jnp.where(first_half, high, low)

    def ext_copy(apart):
        return pltpu.make_async_remote_copy(
            src_ref=ext_out,
            dst_ref=ext_in.at[apart - 1],
            send_sem=ext_send.at[apart - 1],
            recv_sem=ext_recv.at[apart - 1],
            device_id=device_at(apart),
            device_id_type=MESH,
        )

    for_others(lambda apart: ext_copy(apart).start())
    state_v[:rows] = jnp.where(first_half, results[0], pltpu.roll(results[1], half, 1))
    state_v[rows:] = jnp.where(first_half, pltpu.roll(results[0], half, 1), results[1])
    for chunk in range(CHUNKS):
        for apart in range(1, n_wide):
            wide_copy(chunk, apart).wait_send()
        for apart in range(1, n_narrow):
            narrow_copy(chunk, apart).wait_send()
    for_others(lambda apart: ext_copy(apart).wait_recv())
    total = jnp.maximum(ext_out[...], ext_in[...].max(axis=0))
    highest = jnp.max(jnp.where(first_half, total, -jnp.inf), axis=1, keepdims=True)
    lowest = -jnp.max(jnp.where(first_half, -jnp.inf, total), axis=1, keepdims=True)
    middle = (highest + lowest) * 0.5
    halfwidth = (highest - lowest) * 0.5 + 1e-06
    scale = companding / halfwidth
    for plane in range(2):
        values = (state_v[plane * rows : (plane + 1) * rows] - middle) * scale
        magnitude = jnp.abs(values)
        squared = magnitude * magnitude + 1.0
        grown = jnp.log(magnitude + squared * lax.rsqrt(squared)) * (1.0 / companding_norm)
        out_ref[pl.ds(plane, rows, stride=2), :] = jnp.where(values < 0, -grown, grown)
    for_others(lambda apart: ext_copy(apart).wait_send())


def local(state, gates, gate_qubits, swap_order):
    n_wide = lax.axis_size("wide")
    n_narrow = lax.axis_size("narrow")
    upper = state.shape[1].bit_length() - 1 - LANE_QUBITS
    rows = 2**upper
    gate_count, gate_bits = gate_qubits.shape
    gate_dim = 2**gate_bits
    stages = (range(3), range(3, 6), range(6, gate_count))
    dma = pltpu.SemaphoreType.DMA
    woven = state.reshape(2, rows, LANES).transpose(1, 0, 2).reshape(2 * rows, LANES)
    final = pl.pallas_call(
        functools.partial(kernel, n_wide, n_narrow, upper, gate_bits, stages),
        out_shape=jax.ShapeDtypeStruct((2 * rows, LANES), jnp.float32),
        in_specs=[pl.BlockSpec(memory_space=pltpu.HBM)] * 4,
        out_specs=pl.BlockSpec(memory_space=pltpu.VMEM),
        scratch_shapes=[
            pltpu.SMEM(gate_qubits.shape, jnp.int32),
            pltpu.SMEM(swap_order.shape, jnp.int32),
            pltpu.VMEM((2 * rows, LANES), jnp.float32),
            pltpu.VMEM(gates.shape, jnp.float32),
            pltpu.VMEM((gate_count + 3, rows, rows), jnp.bfloat16),
            pltpu.VMEM((gate_count, 2 * gate_dim, 2 * gate_dim), jnp.bfloat16),
            pltpu.VMEM((CHUNKS, n_wide, rows // n_wide, LANES), jnp.float32),
            pltpu.VMEM((CHUNKS, n_wide, rows // n_wide, LANES), jnp.float32),
            pltpu.VMEM((CHUNKS, n_narrow, rows // n_narrow, LANES), jnp.float32),
            pltpu.VMEM((CHUNKS, n_narrow, rows // n_narrow, LANES), jnp.float32),
            pltpu.VMEM((1, LANES), jnp.float32),
            pltpu.VMEM((n_wide * n_narrow - 1, 1, LANES), jnp.float32),
            dma((3,)),
            dma((gate_count,)),
            dma((CHUNKS, n_wide - 1)),
            dma((CHUNKS, n_wide - 1)),
            dma((CHUNKS, n_narrow - 1)),
            dma((CHUNKS, n_narrow - 1)),
            dma((n_wide * n_narrow - 1,)),
            dma((n_wide * n_narrow - 1,)),
        ],
        compiler_params=pltpu.CompilerParams(
            collective_id=0, has_side_effects=True, vmem_limit_bytes=67043328
        ),
        name="gate_layers",
    )(gate_qubits, swap_order, woven, gates)
    return final.reshape(rows, 2, LANES).transpose(1, 0, 2).reshape(state.shape)


def solution(mesh):
    in_specs = (P(None, ("wide", "narrow")), P(), P(), P())
    out_specs = P(None, ("wide", "narrow"))
    return jax.shard_map(local, mesh=mesh, in_specs=in_specs, out_specs=out_specs, check_vma=False)
```

```python
import functools
import math

import jax
import jax.numpy as jnp
from jax import lax
from jax.experimental import pallas as pl
from jax.experimental.pallas import tpu as pltpu
from jax.sharding import PartitionSpec as P

LANE_QUBITS = 7
LANES = 2**LANE_QUBITS
WIDTHS = (LANES // 4, LANES // 2, LANES // 4)
CHUNKS = len(WIDTHS)

companding = 16.0
companding_norm = math.log(16.0 + math.sqrt(257.0))

MESH = pl.DeviceIdType.MESH


def kernel(
    n_wide,
    n_narrow,
    upper,
    gate_bits,
    stages,
    qubits_hbm,
    swap_hbm,
    state_ref,
    gates_ref,
    out_ref,
    curve_ref,
    qubits_ref,
    swap_ref,
    state_v,
    gates_v,
    final_v,
    perms,
    mats,
    *rest_refs,
):
    wide_out, wide_in, narrow_out, narrow_in = (
        rest_refs[k * CHUNKS : (k + 1) * CHUNKS] for k in range(4)
    )
    (
        ext_out,
        ext_in,
        local_sem,
        gate_sem,
        wide_send,
        wide_recv,
        narrow_send,
        narrow_recv,
        ext_send,
        ext_recv,
    ) = rest_refs[4 * CHUNKS :]
    rows = 2**upper
    gate_dim = 2**gate_bits
    rest = rows // gate_dim
    wide_bits = n_wide.bit_length() - 1
    narrow_bits = n_narrow.bit_length() - 1
    wide_me = lax.axis_index("wide")
    narrow_me = lax.axis_index("narrow")
    half = LANES // 2

    qubits_copy = pltpu.make_async_copy(qubits_hbm, qubits_ref, local_sem.at[1])
    qubits_copy.start()
    swap_copy = pltpu.make_async_copy(swap_hbm, swap_ref, local_sem.at[2])
    swap_copy.start()
    state_copy = pltpu.make_async_copy(state_ref, state_v, local_sem.at[0])
    state_copy.start()
    gate_copies = []
    for number in range(gates_v.shape[0]):
        copy = pltpu.make_async_copy(
            gates_ref.at[number], gates_v.at[number], gate_sem.at[number]
        )
        copy.start()
        gate_copies.append(copy)

    barrier = pltpu.get_barrier_semaphore()
    devices = n_wide * n_narrow
    flat_me = wide_me * n_narrow + narrow_me

    def device_at(apart):
        other = lax.rem(flat_me + apart, devices)
        return (lax.div(other, n_narrow), lax.rem(other, n_narrow))

    def for_others(step):
        if devices <= 64:
            for apart in range(1, devices):
                step(apart)
        else:
            lax.fori_loop(1, devices, lambda apart, _: step(apart), None)

    def greet(apart):
        pl.semaphore_signal(barrier, inc=1, device_id=device_at(apart), device_id_type=MESH)

    for_others(greet)
    qubits_copy.wait()
    swap_copy.wait()

    def gate_layout(number):
        masks = [jnp.int32(1) << (qubits_ref[number, k] - LANE_QUBITS) for k in range(gate_bits)]
        left = jnp.int32(rows - 1)
        for mask in masks:
            left = left - mask
        for _ in range(upper - gate_bits):
            low = left & (-left)
            masks.append(low)
            left = left - low
        return masks

    def swap_layout(order):
        return [jnp.int32(1) << (swap_ref[k] - LANE_QUBITS) for k in order]

    natural = [jnp.int32(1 << k) for k in range(upper)]
    wide_layout = swap_layout(range(upper))
    narrow_layout = swap_layout(list(range(narrow_bits, upper)) + list(range(narrow_bits)))

    column = lax.broadcasted_iota(jnp.int32, (1, rows), 1)
    row = lax.broadcasted_iota(jnp.int32, (rows, rows), 0)

    def make_perm(slot, source, target):
        index = jnp.zeros((1, rows), jnp.int32)
        for k in range(upper):
            index = index + jnp.where((column & (1 << k)) != 0, source[k], 0)
        goal = jnp.zeros((1, rows), jnp.int32)
        for k in range(upper):
            goal = goal + jnp.where((index & target[k]) != 0, 1 << k, 0)
        perms[slot] = (row == goal).astype(jnp.float32).astype(jnp.bfloat16)

    def make_matrix(number):
        gate_copies[number].wait()
        whole = jnp.concatenate([gates_v[number, 0], gates_v[number, 1]], axis=1)
        high = whole.astype(jnp.bfloat16)
        low = (whole - high.astype(jnp.float32)).astype(jnp.bfloat16)
        mats[number, :gate_dim] = high
        mats[number, gate_dim:] = low

    lane = lax.broadcasted_iota(jnp.int32, (1, LANES), 1)
    first_half = lane < half

    def permuted(values, slot, width):
        high = values.astype(jnp.bfloat16)
        low = values - high.astype(jnp.float32)
        if width == half:
            both = jnp.concatenate([high, low.astype(jnp.bfloat16)], axis=1)
        else:
            both = jnp.where(first_half, high.astype(jnp.float32), low).astype(jnp.bfloat16)
        return jnp.dot(perms[slot], both, preferred_element_type=jnp.float32)

    def stacked(values, width):
        if width == half:
            turned = pltpu.roll(values, half, 1) * jnp.where(first_half, -1.0, 1.0)
        else:
            turned = jnp.where(
                lax.rem(lane, 2 * width) < width,
                -pltpu.roll(values, LANES - width, 1),
                pltpu.roll(values, width, 1),
            )
        pieces = []
        for part in (values, turned):
            pieces.append(
                jnp.concatenate(
                    [part[k * gate_dim : (k + 1) * gate_dim] for k in range(rest)], axis=1
                ).astype(jnp.bfloat16)
            )
        return jnp.concatenate(pieces, axis=0)

    def gate(values, slot, number, width):
        both = permuted(values, slot, width)
        if width == half:
            first = jnp.dot(
                mats[number], stacked(both[:, :LANES], width), preferred_element_type=jnp.float32
            )
            second = jnp.dot(
                mats[number, :gate_dim],
                stacked(both[:, LANES:], width),
                preferred_element_type=jnp.float32,
            )
            mixed = first[:gate_dim] + (first[gate_dim:] + second)
        else:
            first = jnp.dot(mats[number], stacked(both, width), preferred_element_type=jnp.float32)
            mixed = first[:gate_dim] + first[gate_dim:]
        mixed = jnp.concatenate(
            [mixed[:, k * LANES : (k + 1) * LANES] for k in range(rest)], axis=0
        )
        return mixed if width == half else mixed + pltpu.roll(mixed, half, 1)

    def moved(values, slot, width):
        both = permuted(values, slot, width)
        if width == half:
            return both[:, :LANES] + both[:, LANES:]
        return both + pltpu.roll(both, half, 1)

    def packed(values, blocks, width):
        values = values.reshape(blocks, rows // blocks, LANES)
        if width == half:
            return values
        depth = rows // blocks // 2
        return jnp.where(first_half, values[:, :depth], values[:, depth:])

    def unpacked(values, width):
        if width == half:
            return values.reshape(rows, LANES)
        blocks, depth, _ = values.shape
        turned = pltpu.roll(values.reshape(blocks * depth, LANES), half, 1).reshape(values.shape)
        return jnp.concatenate(
            [jnp.where(first_half, values, turned), jnp.where(first_half, turned, values)], axis=1
        ).reshape(rows, LANES)

    def wide_copy(chunk, apart):
        other = lax.rem(wide_me + apart, n_wide)
        return pltpu.make_async_remote_copy(
            src_ref=wide_out[chunk].at[other],
            dst_ref=wide_in[chunk].at[wide_me],
            send_sem=wide_send.at[chunk, apart - 1],
            recv_sem=wide_recv.at[chunk, apart - 1],
            device_id=(other, narrow_me),
            device_id_type=MESH,
        )

    def narrow_copy(chunk, apart):
        other = lax.rem(narrow_me + apart, n_narrow)
        return pltpu.make_async_remote_copy(
            src_ref=narrow_out[chunk].at[other],
            dst_ref=narrow_in[chunk].at[narrow_me],
            send_sem=narrow_send.at[chunk, apart - 1],
            recv_sem=narrow_recv.at[chunk, apart - 1],
            device_id=(wide_me, other),
            device_id_type=MESH,
        )

    slot = 0
    plan = []
    for numbers, leave in zip(stages, (wide_layout, narrow_layout, natural)):
        plan.append((slot, numbers, leave))
        slot += len(numbers) + 1

    def prepare(stage, layout):
        start, numbers, leave = plan[stage]
        for k, number in enumerate(numbers):
            target = gate_layout(number)
            make_perm(start + k, layout, target)
            make_matrix(number)
            layout = target
        make_perm(start + len(numbers), layout, leave)

    def run(values, stage, width):
        start, numbers, _ = plan[stage]
        for k, number in enumerate(numbers):
            values = gate(values, start + k, number, width)
        return moved(values, start + len(numbers), width)

    def turn(values, by):
        by = by % LANES
        return values if by == 0 else pltpu.roll(values, by, 1)

    firsts = [sum(WIDTHS[:chunk]) for chunk in range(CHUNKS)]

    def piece(chunk):
        width = WIDTHS[chunk]
        values = None
        for group in range(LANES // width):
            part = turn((real, imag)[group % 2], group * width - firsts[chunk])
            values = part if group == 0 else jnp.where(lane < group * width, values, part)
        return values

    prepare(0, natural)
    state_copy.wait()
    real = state_v[pl.ds(0, rows, stride=2), :]
    imag = state_v[pl.ds(1, rows, stride=2), :]
    for chunk, width in enumerate(WIDTHS):
        values = run(piece(chunk), 0, width)
        wide_out[chunk][...] = packed(values, n_wide, width)
        if chunk == 0:
            pl.semaphore_wait(barrier, devices - 1)
        for apart in range(1, n_wide):
            wide_copy(chunk, apart).start()
        wide_in[chunk][wide_me] = wide_out[chunk][wide_me]

    prepare(1, wide_layout)
    prepare(2, narrow_layout)
    for chunk, width in enumerate(WIDTHS):
        for apart in range(1, n_wide):
            wide_copy(chunk, apart).wait_recv()
        values = run(unpacked(wide_in[chunk][...], width), 1, width)
        narrow_out[chunk][...] = packed(values, n_narrow, width)
        for apart in range(1, n_narrow):
            narrow_copy(chunk, apart).start()
        narrow_in[chunk][narrow_me] = narrow_out[chunk][narrow_me]

    results = []
    for chunk, width in enumerate(WIDTHS):
        for apart in range(1, n_narrow):
            narrow_copy(chunk, apart).wait_recv()
        results.append(run(unpacked(narrow_in[chunk][...], width), 2, width))

    high = functools.reduce(jnp.maximum, results).max(axis=0, keepdims=True)
    low = -functools.reduce(jnp.minimum, results).min(axis=0, keepdims=True)
    high = jnp.maximum(high, pltpu.roll(high, half, 1))
    low = jnp.maximum(low, pltpu.roll(low, half, 1))
    ext_out[...] = jnp.where(first_half, high, low)

    def ext_copy(apart):
        return pltpu.make_async_remote_copy(
            src_ref=ext_out,
            dst_ref=ext_in.at[apart - 1],
            send_sem=ext_send.at[apart - 1],
            recv_sem=ext_recv.at[apart - 1],
            device_id=device_at(apart),
            device_id_type=MESH,
        )

    for_others(lambda apart: ext_copy(apart).start())
    for plane in range(2):
        values = None
        for chunk, width in enumerate(WIDTHS):
            part = turn(results[chunk], firsts[chunk] - plane * width)
            values = part if chunk == 0 else jnp.where(lane < firsts[chunk], values, part)
        final_v[pl.ds(plane, rows, stride=2), :] = values
    final_copy = pltpu.make_async_copy(final_v, out_ref, local_sem.at[3])
    final_copy.start()
    for chunk in range(CHUNKS):
        for apart in range(1, n_wide):
            wide_copy(chunk, apart).wait_send()
        for apart in range(1, n_narrow):
            narrow_copy(chunk, apart).wait_send()
    for_others(lambda apart: ext_copy(apart).wait_recv())
    total = jnp.maximum(ext_out[...], ext_in[...].max(axis=0))
    highest = jnp.max(jnp.where(first_half, total, -jnp.inf), axis=1, keepdims=True)
    lowest = -jnp.max(jnp.where(first_half, -jnp.inf, total), axis=1, keepdims=True)
    middle = (highest + lowest) * 0.5
    halfwidth = (highest - lowest) * 0.5 + 1e-06
    curve_ref[...] = jnp.concatenate(
        [jnp.broadcast_to(middle, (4, LANES)), jnp.broadcast_to(companding / halfwidth, (4, LANES))],
        axis=0,
    )
    for_others(lambda apart: ext_copy(apart).wait_send())
    final_copy.wait()


def compand(curve_ref, final_ref, out_ref):
    values = (final_ref[...] - curve_ref[0:1]) * curve_ref[4:5]
    magnitude = jnp.abs(values)
    squared = magnitude * magnitude + 1.0
    grown = jnp.log(magnitude + squared * lax.rsqrt(squared)) * (1.0 / companding_norm)
    out_ref[...] = jnp.where(values < 0, -grown, grown)


def local(state, gates, gate_qubits, swap_order):
    n_wide = lax.axis_size("wide")
    n_narrow = lax.axis_size("narrow")
    upper = state.shape[1].bit_length() - 1 - LANE_QUBITS
    rows = 2**upper
    gate_count, gate_bits = gate_qubits.shape
    gate_dim = 2**gate_bits
    stages = (range(3), range(3, 6), range(6, gate_count))
    dma = pltpu.SemaphoreType.DMA
    woven = state.reshape(2, rows, LANES).transpose(1, 0, 2).reshape(2 * rows, LANES)
    final, curve = pl.pallas_call(
        functools.partial(kernel, n_wide, n_narrow, upper, gate_bits, stages),
        out_shape=(
            jax.ShapeDtypeStruct((2 * rows, LANES), jnp.float32),
            jax.ShapeDtypeStruct((8, LANES), jnp.float32),
        ),
        in_specs=[pl.BlockSpec(memory_space=pltpu.HBM)] * 4,
        out_specs=(pl.BlockSpec(memory_space=pl.ANY), pl.BlockSpec(memory_space=pltpu.VMEM)),
        scratch_shapes=[
            pltpu.SMEM(gate_qubits.shape, jnp.int32),
            pltpu.SMEM(swap_order.shape, jnp.int32),
            pltpu.VMEM((2 * rows, LANES), jnp.float32),
            pltpu.VMEM(gates.shape, jnp.float32),
            pltpu.VMEM((2 * rows, LANES), jnp.float32),
            pltpu.VMEM((gate_count + 3, rows, rows), jnp.bfloat16),
            pltpu.VMEM((gate_count, 2 * gate_dim, 2 * gate_dim), jnp.bfloat16),
            *[
                pltpu.VMEM((blocks, rows // blocks * 2 * width // LANES, LANES), jnp.float32)
                for blocks in (n_wide, n_wide, n_narrow, n_narrow)
                for width in WIDTHS
            ],
            pltpu.VMEM((1, LANES), jnp.float32),
            pltpu.VMEM((n_wide * n_narrow - 1, 1, LANES), jnp.float32),
            dma((4,)),
            dma((gate_count,)),
            dma((CHUNKS, n_wide - 1)),
            dma((CHUNKS, n_wide - 1)),
            dma((CHUNKS, n_narrow - 1)),
            dma((CHUNKS, n_narrow - 1)),
            dma((n_wide * n_narrow - 1,)),
            dma((n_wide * n_narrow - 1,)),
        ],
        compiler_params=pltpu.CompilerParams(
            collective_id=0, has_side_effects=True, vmem_limit_bytes=67043328
        ),
        name="gate_layers",
    )(gate_qubits, swap_order, woven, gates)
    steps = 4
    block = pl.BlockSpec((2 * rows // steps, LANES), lambda step: (step, 0))
    final = pl.pallas_call(
        compand,
        grid=(steps,),
        out_shape=jax.ShapeDtypeStruct((2 * rows, LANES), jnp.float32),
        in_specs=[pl.BlockSpec((8, LANES), lambda step: (0, 0)), block],
        out_specs=block,
        name="compand",
    )(curve, final)
    return final.reshape(rows, 2, LANES).transpose(1, 0, 2).reshape(state.shape)


def solution(mesh):
    in_specs = (P(None, ("wide", "narrow")), P(), P(), P())
    out_specs = P(None, ("wide", "narrow"))
    return jax.shard_map(local, mesh=mesh, in_specs=in_specs, out_specs=out_specs, check_vma=False)
```

```python
import functools
import math

import jax
import jax.numpy as jnp
from jax import lax
from jax.experimental import pallas as pl
from jax.experimental.pallas import tpu as pltpu
from jax.sharding import PartitionSpec as P

LANE_QUBITS = 7
LANES = 2**LANE_QUBITS
CHUNKS = 2

companding = 16.0
companding_norm = math.log(16.0 + math.sqrt(257.0))

MESH = pl.DeviceIdType.MESH


def kernel(
    n_wide,
    n_narrow,
    upper,
    gate_bits,
    stages,
    qubits_hbm,
    swap_hbm,
    state_ref,
    gates_ref,
    out_ref,
    qubits_ref,
    swap_ref,
    state_v,
    gates_v,
    perms,
    mats,
    wide_out,
    wide_in,
    narrow_out,
    narrow_in,
    ext_out,
    ext_in,
    local_sem,
    gate_sem,
    wide_send,
    wide_recv,
    narrow_send,
    narrow_recv,
    ext_send,
    ext_recv,
):
    rows = 2**upper
    gate_dim = 2**gate_bits
    rest = rows // gate_dim
    wide_bits = n_wide.bit_length() - 1
    narrow_bits = n_narrow.bit_length() - 1
    wide_me = lax.axis_index("wide")
    narrow_me = lax.axis_index("narrow")
    half = LANES // 2

    qubits_copy = pltpu.make_async_copy(qubits_hbm, qubits_ref, local_sem.at[1])
    qubits_copy.start()
    swap_copy = pltpu.make_async_copy(swap_hbm, swap_ref, local_sem.at[2])
    swap_copy.start()
    state_copy = pltpu.make_async_copy(state_ref, state_v, local_sem.at[0])
    state_copy.start()
    gate_copies = []
    for number in range(gates_v.shape[0]):
        copy = pltpu.make_async_copy(
            gates_ref.at[number], gates_v.at[number], gate_sem.at[number]
        )
        copy.start()
        gate_copies.append(copy)

    barrier = pltpu.get_barrier_semaphore()
    devices = n_wide * n_narrow
    flat_me = wide_me * n_narrow + narrow_me

    def device_at(apart):
        other = lax.rem(flat_me + apart, devices)
        return (lax.div(other, n_narrow), lax.rem(other, n_narrow))

    def for_others(step):
        if devices <= 64:
            for apart in range(1, devices):
                step(apart)
        else:
            lax.fori_loop(1, devices, lambda apart, _: step(apart), None)

    def greet(apart):
        pl.semaphore_signal(barrier, inc=1, device_id=device_at(apart), device_id_type=MESH)

    for_others(greet)
    qubits_copy.wait()
    swap_copy.wait()

    def gate_layout(number):
        masks = [jnp.int32(1) << (qubits_ref[number, k] - LANE_QUBITS) for k in range(gate_bits)]
        left = jnp.int32(rows - 1)
        for mask in masks:
            left = left - mask
        for _ in range(upper - gate_bits):
            low = left & (-left)
            masks.append(low)
            left = left - low
        return masks

    def swap_layout(order):
        return [jnp.int32(1) << (swap_ref[k] - LANE_QUBITS) for k in order]

    natural = [jnp.int32(1 << k) for k in range(upper)]
    wide_layout = swap_layout(range(upper))
    narrow_layout = swap_layout(list(range(narrow_bits, upper)) + list(range(narrow_bits)))

    column = lax.broadcasted_iota(jnp.int32, (1, rows), 1)
    row = lax.broadcasted_iota(jnp.int32, (rows, rows), 0)

    def make_perm(slot, source, target):
        index = jnp.zeros((1, rows), jnp.int32)
        for k in range(upper):
            index = index + jnp.where((column & (1 << k)) != 0, source[k], 0)
        goal = jnp.zeros((1, rows), jnp.int32)
        for k in range(upper):
            goal = goal + jnp.where((index & target[k]) != 0, 1 << k, 0)
        perms[slot] = (row == goal).astype(jnp.float32).astype(jnp.bfloat16)

    def make_matrix(number):
        gate_copies[number].wait()
        whole = jnp.concatenate([gates_v[number, 0], gates_v[number, 1]], axis=1)
        high = whole.astype(jnp.bfloat16)
        low = (whole - high.astype(jnp.float32)).astype(jnp.bfloat16)
        mats[number, :gate_dim] = high
        mats[number, gate_dim:] = low

    sign = jnp.where(lax.broadcasted_iota(jnp.int32, (1, LANES), 1) < half, -1.0, 1.0)

    def permuted(values, slot):
        high = values.astype(jnp.bfloat16)
        low = (values - high.astype(jnp.float32)).astype(jnp.bfloat16)
        both = jnp.concatenate([high, low], axis=1)
        moved = jnp.dot(perms[slot], both, preferred_element_type=jnp.float32)
        return moved[:, :LANES], moved[:, LANES:]

    def gate(values, slot, number):
        both = jnp.concatenate(permuted(values, slot), axis=1)
        blocks = []
        for k in range(rest):
            part = both[k * gate_dim : (k + 1) * gate_dim]
            turned = jnp.concatenate(
                [
                    pltpu.roll(part[:, :LANES], half, 1) * sign,
                    pltpu.roll(part[:, LANES:], half, 1) * sign,
                ],
                axis=1,
            )
            whole = jnp.concatenate([part, turned], axis=0).astype(jnp.bfloat16)
            mixed = jnp.dot(mats[number], whole, preferred_element_type=jnp.float32)
            blocks.append(
                mixed[:gate_dim, :LANES]
                + (mixed[gate_dim:, :LANES] + mixed[:gate_dim, LANES:])
            )
        return jnp.concatenate(blocks, axis=0)

    def moved(values, slot):
        high, low = permuted(values, slot)
        return high + low

    def wide_copy(chunk, apart):
        other = lax.rem(wide_me + apart, n_wide)
        return pltpu.make_async_remote_copy(
            src_ref=wide_out.at[chunk, other],
            dst_ref=wide_in.at[chunk, wide_me],
            send_sem=wide_send.at[chunk, apart - 1],
            recv_sem=wide_recv.at[chunk, apart - 1],
            device_id=(other, narrow_me),
            device_id_type=MESH,
        )

    def narrow_copy(chunk, apart):
        other = lax.rem(narrow_me + apart, n_narrow)
        return pltpu.make_async_remote_copy(
            src_ref=narrow_out.at[chunk, other],
            dst_ref=narrow_in.at[chunk, narrow_me],
            send_sem=narrow_send.at[chunk, apart - 1],
            recv_sem=narrow_recv.at[chunk, apart - 1],
            device_id=(wide_me, other),
            device_id_type=MESH,
        )

    slot = 0
    plan = []
    for numbers, leave in zip(stages, (wide_layout, narrow_layout, natural)):
        plan.append((slot, numbers, leave))
        slot += len(numbers) + 1

    def prepare(stage, layout):
        start, numbers, leave = plan[stage]
        for k, number in enumerate(numbers):
            target = gate_layout(number)
            make_perm(start + k, layout, target)
            make_matrix(number)
            layout = target
        make_perm(start + len(numbers), layout, leave)

    def run(values, stage):
        start, numbers, _ = plan[stage]
        for k, number in enumerate(numbers):
            values = gate(values, start + k, number)
        return moved(values, start + len(numbers))

    prepare(0, natural)
    state_copy.wait()
    real = state_v[pl.ds(0, rows, stride=2), :]
    imag = state_v[pl.ds(1, rows, stride=2), :]
    first_half = lax.broadcasted_iota(jnp.int32, (1, LANES), 1) < half
    pieces = (
        jnp.where(first_half, real, pltpu.roll(imag, half, 1)),
        jnp.where(first_half, pltpu.roll(real, half, 1), imag),
    )
    for chunk in range(CHUNKS):
        values = run(pieces[chunk], 0)
        wide_out[chunk] = values.reshape(n_wide, rows // n_wide, LANES)
        if chunk == 0:
            pl.semaphore_wait(barrier, devices - 1)
        for apart in range(1, n_wide):
            wide_copy(chunk, apart).start()
        wide_in[chunk, wide_me] = wide_out[chunk, wide_me]

    prepare(1, wide_layout)
    prepare(2, narrow_layout)
    for chunk in range(CHUNKS):
        for apart in range(1, n_wide):
            wide_copy(chunk, apart).wait_recv()
        values = run(wide_in[chunk].reshape(rows, LANES), 1)
        narrow_out[chunk] = values.reshape(n_narrow, rows // n_narrow, LANES)
        for apart in range(1, n_narrow):
            narrow_copy(chunk, apart).start()
        narrow_in[chunk, narrow_me] = narrow_out[chunk, narrow_me]

    results = []
    for chunk in range(CHUNKS):
        for apart in range(1, n_narrow):
            narrow_copy(chunk, apart).wait_recv()
        results.append(run(narrow_in[chunk].reshape(rows, LANES), 2))

    high = jnp.maximum(results[0], results[1]).max(axis=0, keepdims=True)
    low = -jnp.minimum(results[0], results[1]).min(axis=0, keepdims=True)
    high = jnp.maximum(high, pltpu.roll(high, half, 1))
    low = jnp.maximum(low, pltpu.roll(low, half, 1))
    ext_out[...] = jnp.where(first_half, high, low)

    def ext_copy(apart):
        return pltpu.make_async_remote_copy(
            src_ref=ext_out,
            dst_ref=ext_in.at[apart - 1],
            send_sem=ext_send.at[apart - 1],
            recv_sem=ext_recv.at[apart - 1],
            device_id=device_at(apart),
            device_id_type=MESH,
        )

    for_others(lambda apart: ext_copy(apart).start())
    state_v[:rows] = jnp.where(first_half, results[0], pltpu.roll(results[1], half, 1))
    state_v[rows:] = jnp.where(first_half, pltpu.roll(results[0], half, 1), results[1])
    for chunk in range(CHUNKS):
        for apart in range(1, n_wide):
            wide_copy(chunk, apart).wait_send()
        for apart in range(1, n_narrow):
            narrow_copy(chunk, apart).wait_send()
    for_others(lambda apart: ext_copy(apart).wait_recv())
    total = jnp.maximum(ext_out[...], ext_in[...].max(axis=0))
    highest = jnp.max(jnp.where(first_half, total, -jnp.inf), axis=1, keepdims=True)
    lowest = -jnp.max(jnp.where(first_half, -jnp.inf, total), axis=1, keepdims=True)
    middle = (highest + lowest) * 0.5
    halfwidth = (highest - lowest) * 0.5 + 1e-06
    scale = companding / halfwidth
    for plane in range(2):
        values = (state_v[plane * rows : (plane + 1) * rows] - middle) * scale
        magnitude = jnp.abs(values)
        squared = magnitude * magnitude + 1.0
        grown = jnp.log(magnitude + squared * lax.rsqrt(squared)) * (1.0 / companding_norm)
        out_ref[pl.ds(plane, rows, stride=2), :] = jnp.where(values < 0, -grown, grown)
    for_others(lambda apart: ext_copy(apart).wait_send())


def local(state, gates, gate_qubits, swap_order):
    n_wide = lax.axis_size("wide")
    n_narrow = lax.axis_size("narrow")
    upper = state.shape[1].bit_length() - 1 - LANE_QUBITS
    rows = 2**upper
    gate_count, gate_bits = gate_qubits.shape
    gate_dim = 2**gate_bits
    stages = (range(3), range(3, 6), range(6, gate_count))
    dma = pltpu.SemaphoreType.DMA
    woven = state.reshape(2, rows, LANES).transpose(1, 0, 2).reshape(2 * rows, LANES)
    final = pl.pallas_call(
        functools.partial(kernel, n_wide, n_narrow, upper, gate_bits, stages),
        out_shape=jax.ShapeDtypeStruct((2 * rows, LANES), jnp.float32),
        in_specs=[pl.BlockSpec(memory_space=pltpu.HBM)] * 4,
        out_specs=pl.BlockSpec(memory_space=pltpu.VMEM),
        scratch_shapes=[
            pltpu.SMEM(gate_qubits.shape, jnp.int32),
            pltpu.SMEM(swap_order.shape, jnp.int32),
            pltpu.VMEM((2 * rows, LANES), jnp.float32),
            pltpu.VMEM(gates.shape, jnp.float32),
            pltpu.VMEM((gate_count + 3, rows, rows), jnp.bfloat16),
            pltpu.VMEM((gate_count, 2 * gate_dim, 2 * gate_dim), jnp.bfloat16),
            pltpu.VMEM((CHUNKS, n_wide, rows // n_wide, LANES), jnp.float32),
            pltpu.VMEM((CHUNKS, n_wide, rows // n_wide, LANES), jnp.float32),
            pltpu.VMEM((CHUNKS, n_narrow, rows // n_narrow, LANES), jnp.float32),
            pltpu.VMEM((CHUNKS, n_narrow, rows // n_narrow, LANES), jnp.float32),
            pltpu.VMEM((1, LANES), jnp.float32),
            pltpu.VMEM((n_wide * n_narrow - 1, 1, LANES), jnp.float32),
            dma((3,)),
            dma((gate_count,)),
            dma((CHUNKS, n_wide - 1)),
            dma((CHUNKS, n_wide - 1)),
            dma((CHUNKS, n_narrow - 1)),
            dma((CHUNKS, n_narrow - 1)),
            dma((n_wide * n_narrow - 1,)),
            dma((n_wide * n_narrow - 1,)),
        ],
        compiler_params=pltpu.CompilerParams(
            collective_id=0, has_side_effects=True, vmem_limit_bytes=67043328
        ),
        name="gate_layers",
    )(gate_qubits, swap_order, woven, gates)
    return final.reshape(rows, 2, LANES).transpose(1, 0, 2).reshape(state.shape)


def solution(mesh):
    in_specs = (P(None, ("wide", "narrow")), P(), P(), P())
    out_specs = P(None, ("wide", "narrow"))
    return jax.shard_map(local, mesh=mesh, in_specs=in_specs, out_specs=out_specs, check_vma=False)
```
